512 devices in a mesh: grp: 16 (over z, core), blk: 32 (over y, x).
Axes of the slice: x: 4, y: 8, z: 8, core: 2. Of those that a mesh axis runs over, the one named last changes fastest.
Arguments:
- tile_values: bfloat16 [16384, 320, 128], P(('grp', 'blk'))
- tile_paper: int32 [16384], P(('grp', 'blk')), may hold values from 0 to 1
- tile_author: int32 [16384], P(('grp', 'blk')), may hold values from 0 to 1
- tile_count: int32 [512], P(('grp', 'blk')), may hold values from 8 to 32, as said below
- seed_class: int32 [327680], P(('grp', 'blk')), may hold values from 0 to 152
- train_mask: int32 [327680], P(('grp', 'blk')), may hold values from 0 to 1
- class_prior: float32 [256], replicated, may hold values from 0.02 to 0.2
- class_target: float32 [256], replicated, may hold values from 0.5 to 2
Outputs:
- paper_scores: float32 [327680, 256], P(('grp', 'blk'))
- author_scores: float32 [131072, 256], P(('grp', 'blk'))
The draws below stay inside these ranges and needn't reach their ends.
Inputs may be any that keep to these rules, and one draw needn't show every extreme that they name: The first tile_count[d] slots of device d are live, the others empty; some device has all 32 live.
All inputs are finite; a program needn't handle non-finite values.
Results may differ from the reference program's by a relative error of at most 0.0012.
Values may be sent and summed in bfloat16 or wider, within the bound.
A program may use at most 64 MiB of HBM per device.

```python
import math
import jax
import jax.numpy as jnp
from jax import lax

CLASSES = 256
TP = 320
TA = 128
PT_DEV = 2
AT_DEV = 2
SLOT_PEER = 1
ITERS = 4
ROUNDS = 2
SLOTS = 32
PAPERS = 327680
AUTHORS = 131072
N_GRP = 16
N_BLK = 32
DEVICES = 512


def draw_tile_values(key, part):
    key_value, key_scale = jax.random.split(key)
    row_total = DEVICES * SLOTS
    base_values = jax.random.uniform(key_value, (row_total, TP, TA), jnp.float32, 0.2, 1.0)
    row_scale = jnp.exp(jax.random.uniform(key_scale, (row_total, TP, 1), jnp.float32, 0.0, jnp.log(10.0)))
    device_ramp = 1.0 + 2.0 * (jnp.arange(row_total) // SLOTS).astype(jnp.float32) / max(DEVICES - 1, 1)
    return (base_values * row_scale * device_ramp[:, None, None] * (16.0 / TA)).astype(jnp.bfloat16)


def draw_tile_count(key, part):
    lowest = max(SLOTS // 4, 1)
    counts = jax.random.randint(key, (DEVICES,), lowest, SLOTS + 1)
    return counts.at[0].set(SLOTS).at[1].set(lowest).astype(jnp.int32)


def draw_seed_class(key, part):
    class_total = min(153, CLASSES)
    group_width = SLOTS // SLOT_PEER
    group_total = DEVICES // group_width
    device_papers = PT_DEV * TP
    key_center, key_offset, key_inside = jax.random.split(jax.random.fold_in(key, 11), 3)
    group_center = jax.random.randint(key_center, (group_total,), 0, class_total)
    device_offset = jax.random.randint(key_offset, (DEVICES,), 0, max(class_total // 8, 1))
    inside = jax.random.randint(key_inside, (DEVICES, device_papers), 0, max(class_total // 16, 2))
    device_group = jnp.arange(DEVICES) // group_width
    band_start = group_center[device_group] + device_offset
    classes = (band_start[:, None] + inside) % class_total
    flattened = classes.reshape(DEVICES * device_papers)
    return flattened.at[0].set(class_total - 1).at[1].set(0).astype(jnp.int32)


def draw_train_mask(key, part):
    device_papers = PT_DEV * TP
    key_level, key_value = jax.random.split(jax.random.fold_in(key, 23))
    levels = jax.random.randint(key_level, (DEVICES,), 0, 5).at[0].set(4).at[1].set(1)
    picks = jax.random.randint(key_value, (DEVICES, device_papers), 0, 4)
    return (picks < levels[:, None]).astype(jnp.int32).reshape(DEVICES * device_papers)


def set_ends(array, key, least, high):
    longest = array.shape.index(max(array.shape))
    spots = []
    for shift in (0, 1):
        where = [jax.random.randint(jax.random.fold_in(key, axis), (), 0, length) for axis, length in enumerate(array.shape)]
        where[longest] = (where[longest] + shift) % array.shape[longest]
        spots.append(tuple(where))
    return array.at[spots[0]].set(least).at[spots[1]].set(high)


def setup_inputs(seed: int = 0) -> dict:
    streams_of = jax.random.split(jax.random.key(seed), 9)
    return {
        "tile_values": draw_tile_values(jax.random.fold_in(streams_of[8], 71), 0),
        "tile_paper": set_ends(jax.random.randint(streams_of[1], (DEVICES * SLOTS,), 0, PT_DEV), jax.random.fold_in(streams_of[1], 1), 0, PT_DEV - 1).astype(jnp.int32),
        "tile_author": set_ends(jax.random.randint(streams_of[2], (DEVICES * SLOTS,), 0, AT_DEV), jax.random.fold_in(streams_of[2], 1), 0, AT_DEV - 1).astype(jnp.int32),
        "tile_count": draw_tile_count(jax.random.fold_in(streams_of[8], 71), 0),
        "seed_class": draw_seed_class(jax.random.fold_in(streams_of[8], 71), 0),
        "train_mask": draw_train_mask(jax.random.fold_in(streams_of[8], 71), 0),
        "class_prior": jnp.clip(jnp.exp(jax.random.uniform(streams_of[6], (CLASSES,), jnp.float32, math.log(0.02), math.log(0.2))), 0.02, 0.2),
        "class_target": jnp.clip(jnp.exp(jax.random.uniform(streams_of[7], (CLASSES,), jnp.float32, math.log(0.5), math.log(2.0))), 0.5, 2.0),
    }


keep_share = 0.8


def class_balancer(label_masses, class_prior, class_target):
    kernel = label_masses + class_prior[None, :]
    scale_rows = jnp.ones((kernel.shape[0],), jnp.float32)
    scale_cols = jnp.ones((kernel.shape[1],), jnp.float32)
    for iteration in range(ITERS):
        column = jnp.sum(scale_rows[:, None] * kernel, axis=0)
        scale_cols = class_target / column
        scale_rows = 1.0 / jnp.sum(kernel * scale_cols[None, :], axis=1)
    return scale_rows[:, None] * kernel * scale_cols[None, :]


def reference(tile_values, tile_paper, tile_author, tile_count, seed_class, train_mask, class_prior, class_target):
    slot_count = SLOT_PEER * N_BLK
    high = lax.Precision.HIGHEST
    seed_rows = ((seed_class[:, None] == jnp.arange(CLASSES)[None, :]) & (train_mask[:, None] == 1)).astype(jnp.float32)
    labels = seed_rows.astype(jnp.bfloat16)
    tiles_all = tile_values.reshape(N_GRP, N_BLK, slot_count, TP, TA)
    paper_index = tile_paper.reshape(N_GRP, N_BLK, slot_count)
    author_index = tile_author.reshape(N_GRP, N_BLK, slot_count)
    live_slots = (jnp.arange(slot_count)[None, :] < tile_count[:, None]).astype(jnp.float32).reshape(N_GRP, N_BLK, slot_count)
    target_index = ((jnp.arange(slot_count) // SLOT_PEER)[None, None, :] * AT_DEV + author_index).astype(jnp.int32)
    updated = seed_rows
    author_share = jnp.zeros((AUTHORS, CLASSES), jnp.float32)
    for repeat in range(ROUNDS):
        label_tiles = labels.reshape(N_GRP, N_BLK, PT_DEV, TP, CLASSES)

        def forward(operands):
            tiles_group, label_group, paper_group, target_group, live_group = operands
            chosen = jax.vmap(lambda lookup_table, index_array: lookup_table[index_array])(label_group, paper_group)
            partial_value = jnp.einsum("bspa,bspc->bsac", tiles_group.astype(jnp.float32), chosen.astype(jnp.float32), precision=high)
            parcel = (partial_value * live_group[:, :, None, None]).astype(jnp.bfloat16)
            onehot = (target_group[:, :, None] == jnp.arange(N_BLK * AT_DEV)[None, None, :]).astype(jnp.float32)
            return jnp.einsum("bsk,bsac->kac", onehot, parcel.astype(jnp.float32), precision=high)

        author_mass = lax.map(forward, (tiles_all, label_tiles, paper_index, target_index, live_slots))
        author_mass = author_mass.reshape(AUTHORS, CLASSES)
        author_share = class_balancer(author_mass, class_prior, class_target)
        author_class_labels = author_share.astype(jnp.bfloat16).reshape(N_GRP, N_BLK * AT_DEV, TA, CLASSES)

        def backward(operands):
            tiles_group, authors_group, paper_group, target_group, live_group = operands
            returned = authors_group[target_group]
            products = jnp.einsum("bspa,bsac->bspc", tiles_group.astype(jnp.float32), returned.astype(jnp.float32), precision=high)
            onehot = (paper_group[:, :, None] == jnp.arange(PT_DEV)[None, None, :]).astype(jnp.float32) * live_group[:, :, None]
            return jnp.einsum("bsq,bspc->bqpc", onehot, products, precision=high)

        paper_mass = lax.map(backward, (tiles_all, author_class_labels, paper_index, target_index, live_slots))
        paper_mass = paper_mass.reshape(PAPERS, CLASSES)
        paper_share = class_balancer(paper_mass, class_prior, class_target)
        updated = keep_share * paper_share + (1.0 - keep_share) * seed_rows
        labels = updated.astype(jnp.bfloat16)
    return CLASSES * updated, CLASSES * author_share
```

```python
import functools
import itertools

import jax
import jax.numpy as jnp
from jax import lax
from jax.experimental import pallas as pl
from jax.experimental.pallas import tpu as pltpu
from jax.sharding import PartitionSpec as P

ITERS = 4
ROUNDS = 2
SEED_CLASSES = 160
KEEP = 0.8
MESH = pl.DeviceIdType.MESH
NX, NY, NZ, NC = 4, 8, 8, 2
F32, BF16 = jnp.float32, jnp.bfloat16


def add(terms):
    return functools.reduce(lambda a, b: a + b, terms)


def by_distance(sizes):
    offsets = [o for o in itertools.product(*map(range, sizes)) if any(o)]
    return sorted(offsets, key=lambda o: -sum(min(k, n - k) for k, n in zip(o, sizes)))


YX = by_distance((NY, NX))
ZC = by_distance((NZ, NC))


def kernel(
    tiles_hbm, pick_paper, pick_author, count, code, prior_ref, target_ref,
    paper_out, author_out,
    tiles, masked, labels_t, seeds, labels, degree, weights, author_k, paper_k,
    px, xr, ys0, yr0, ys1, yr1, own, yb, xs, xa,
    sum1, got1, sum2, got2,
    tile_sem, w_send, w_recv, xr_sem, xs_send, yr_sem, ys_send, yb_sem, yb_send, xa_sem, xa_send,
    ss1, rs1, ss2, rs2,
):
    slots, tile_rows, tile_cols = tiles_hbm.shape
    classes = prior_ref.shape[1]
    g, b = lax.axis_index("grp"), lax.axis_index("blk")
    z, c, y, x = lax.div(g, NC), lax.rem(g, NC), lax.div(b, NX), lax.rem(b, NX)

    def at(dy=0, dx=0):
        return (g, lax.rem(y + dy, NY) * NX + lax.rem(x + dx, NX))

    def across(dz, dc):
        return (lax.rem(z + dz, NZ) * NC + lax.rem(c + dc, NC), b)

    def send(src, dst, send_sem, recv_sem, device):
        pltpu.make_async_remote_copy(
            src_ref=src, dst_ref=dst, send_sem=send_sem, recv_sem=recv_sem,
            device_id=device, device_id_type=MESH,
        ).start()

    def drain(ref, sem):
        pltpu.make_async_copy(ref, ref, sem).wait()

    def sum_start(k, row):
        sum1[k] = row
        for j, (dz, dc) in enumerate(ZC):
            send(sum1.at[k], got1.at[k, j], ss1.at[k], rs1.at[k], across(dz, dc))

    def sum_middle(k):
        drain(got1.at[k], rs1.at[k])
        sum2[k] = sum1[k] + jnp.sum(got1[k], axis=0)
        for j, (dy, dx) in enumerate(YX):
            send(sum2.at[k], got2.at[k, j], ss2.at[k], rs2.at[k], at(dy, dx))

    def sum_end(k):
        drain(got2.at[k], rs2.at[k])
        return target_ref[...] / (sum2[k] + jnp.sum(got2[k], axis=0))

    ys, yr = (ys0, ys1), (yr0, yr1)
    load = pltpu.make_async_copy(tiles_hbm, tiles, tile_sem)
    load.start()
    barrier = pltpu.get_barrier_semaphore()
    for dy, dx in YX:
        pl.semaphore_signal(barrier, inc=1, device_id=at(dy, dx), device_id_type=MESH)
    for dz, dc in ZC:
        pl.semaphore_signal(barrier, inc=1, device_id=across(dz, dc), device_id_type=MESH)

    def slot_weights(s, carry):
        live = jnp.where(s < count[0], 1.0, 0.0)
        second = jnp.where(pick_author[s] == 1, 1.0, 0.0)
        for t, value in enumerate(((1.0 - second) * live, second * live, second)):
            weights[0, t, s] = jnp.full((1, classes), value, F32)
        return carry

    lax.fori_loop(0, slots, slot_weights, 0)
    for q in range(2):
        row = lax.broadcasted_iota(jnp.int32, (classes, code.shape[1]), 0)
        hot = jnp.where(row == code[pl.ds(q, 1), :], 1.0, 0.0)
        labels_t[q] = hot.astype(BF16)
        seeds[q] = hot.T[:tile_rows]
        labels[q] = seeds[q]
    pl.semaphore_wait(barrier, len(YX) + len(ZC))
    for dx in range(1, NX):
        send(weights.at[0], weights.at[dx], w_send, w_recv, at(0, dx))
    load.wait()

    def far_first(i):
        half = lax.div(i + 1, 2)
        return 4 + half - 2 * half * lax.rem(i, 2)

    def slot_of(oy, dx):
        return lax.rem(y + oy, NY) * NX + lax.rem(x + dx, NX)

    def forward(r, rows, between, middle, last):
        def parcels(i, carry):
            oy = far_first(i)
            for dx in (2, 1, 3, 0):
                s = slot_of(oy, dx)
                value = jnp.dot(
                    labels_t[pick_paper[s], :rows, :tile_rows], tiles[s], preferred_element_type=F32
                )
                px[r, oy, dx, :rows] = value.astype(BF16)
                if dx:
                    send(
                        px.at[r, oy, dx, pl.ds(0, rows)], xr.at[r, oy, dx - 1, pl.ds(0, rows)],
                        xs_send.at[r], xr_sem.at[r, oy], at(0, dx),
                    )
            return carry

        lax.fori_loop(0, NY, parcels, 0)
        between()

        def row_sums(oy):
            drain(xr.at[r, oy, :, pl.ds(0, rows)], xr_sem.at[r, oy])
            s = slot_of(oy, 0)
            parts = [px[r, oy, 0, :rows].astype(F32)]
            parts += [xr[r, oy, dx - 1, :rows].astype(F32) for dx in range(1, NX)]
            return [
                add(part * weights[dx, t, s][:, :tile_cols] for dx, part in enumerate(parts)) for t in range(2)
            ]

        def onward(i, carry):
            oy = far_first(i)
            for t, total in enumerate(row_sums(oy)):
                ys[r][oy, t, :rows] = total.astype(ys[r].dtype)
            send(
                ys[r].at[oy, :, pl.ds(0, rows)], yr[r].at[oy - 1, :, pl.ds(0, rows)],
                ys_send.at[r], yr_sem.at[r], at(oy, 0),
            )
            return carry

        lax.fori_loop(0, 4, onward, 0)
        middle()
        lax.fori_loop(4, NY - 1, onward, 0)
        totals = row_sums(0)
        first = last()
        drain(yr[r].at[:, :, pl.ds(0, rows)], yr_sem.at[r])
        for t, total in enumerate(totals):
            for j in range(NY - 1):
                total = total + yr[r][j, t, :rows].astype(F32)
            if rows < classes:
                total = jnp.concatenate([total, jnp.zeros((classes - rows, tile_cols), F32)], axis=0)
            k = total.T + prior_ref[...]
            author_k[pl.ds(t * tile_cols, tile_cols), :] = k
            own[r, t] = k.astype(BF16)
        return first

    def mask_tiles():
        degree[...] = jnp.zeros_like(degree)

        def row(oy, carry):
            for dx in range(NX):
                s = slot_of(oy, (NX - dx) % NX)
                live = jnp.where(s < count[0], 1.0, 0.0)
                for q in range(2):
                    keep = jnp.where(pick_paper[s] == q, live, 0.0)
                    part = tiles[s] * jnp.full((1, tile_cols), keep, F32).astype(BF16)
                    masked[q, oy, :, dx * tile_cols:(dx + 1) * tile_cols] = part
                    degree[q] += part.astype(F32)
            return carry

        lax.fori_loop(0, NY, row, 0)

    def first_author_sum():
        nodes = 2.0 * tile_cols
        sums = [
            jnp.sum(jnp.sum(degree[q], axis=1, keepdims=True) * labels[q], axis=0, keepdims=True) for q in range(2)
        ]
        return sums[0] + sums[1] + nodes * prior_ref[...]

    def spread_start(r):
        for d in (4, 3, 5, 2, 6, 1, 7):
            send(own.at[r], yb.at[r, NY - d - 1], yb_send.at[r], yb_sem.at[r, NY - d - 1], at(d, 0))

    def spread(r, oy, both):
        s = slot_of(oy, 0)
        for dx in (2, 1, 3, 0):
            second = weights[(NX - dx) % NX, 2, s] > 0.5
            chosen = jnp.where(second, both[1].astype(F32), both[0].astype(F32))
            if dx:
                xs[r, oy, dx - 1] = chosen.astype(BF16)
                send(xs.at[r, oy, dx - 1], xa.at[r, oy, dx], xa_send.at[r], xa_sem.at[r, oy], at(0, dx))
            else:
                xa[r, oy, 0] = chosen.astype(BF16)

    def spread_far(r, first, stop):
        def step(i, carry):
            oy = far_first(i)
            drain(yb.at[r, oy - 1], yb_sem.at[r, oy - 1])
            spread(r, oy, [yb[r, oy - 1, 0], yb[r, oy - 1, 1]])
            return carry

        lax.fori_loop(first, stop, step, 0)

    def paper_masses(r, columns):
        for q in range(2):
            paper_k[q] = jnp.broadcast_to(prior_ref[...], (tile_rows, classes))

        def step(oy, carry):
            drain(xa.at[r, oy, pl.ds(1, NX - 1)], xa_sem.at[r, oy])
            scaled = xa[r, oy].astype(F32).reshape(NX * tile_cols, classes) * columns
            share = (scaled * (1.0 / jnp.sum(scaled, axis=1, keepdims=True))).astype(BF16)
            for q in range(2):
                paper_k[q] += jnp.dot(masked[q, oy], share, preferred_element_type=F32)
            return carry

        lax.fori_loop(0, NY, step, 0)

    def sum_all(k, row):
        sum_start(k, row)
        sum_middle(k)
        return sum_end(k)

    def rows_of(k, columns):
        return 1.0 / jnp.sum(k * columns, axis=1, keepdims=True)

    for r in range(ROUNDS):
        base = r * 2 * ITERS
        final = r == ROUNDS - 1

        def between():
            if r == 0:
                mask_tiles()
                drain(weights.at[pl.ds(1, NX - 1)], w_recv)
            sum_start(base, first_author_sum())

        columns = forward(
            r, SEED_CLASSES if r == 0 else classes, between, lambda: sum_middle(base), lambda: sum_end(base)
        )
        spread_start(r)
        spread(r, 0, [own[r, 0], own[r, 1]])
        for i in range(1, ITERS):
            k = author_k[...]
            columns = sum_all(base + i, jnp.sum(k * rows_of(k, columns), axis=0, keepdims=True))
            if i == 1:
                spread_far(r, 0, 3)
            if i == 2:
                spread_far(r, 3, NY - 1)
        if final:
            k = author_k[...]
            author_out[...] = classes * (rows_of(k, columns) * k * columns)
        paper_masses(r, columns)
        columns = sum_all(base + ITERS, add(jnp.sum(paper_k[q], axis=0, keepdims=True) for q in range(2)))

        def iterate(i, columns):
            row = add(
                jnp.sum(paper_k[q] * rows_of(paper_k[q], columns), axis=0, keepdims=True) for q in range(2)
            )
            return sum_all(base + ITERS + i, row)

        columns = lax.fori_loop(1, ITERS, iterate, columns)
        for q in range(2):
            k = paper_k[q]
            updated = KEEP * (rows_of(k, columns) * k * columns) + (1.0 - KEEP) * seeds[q]
            if final:
                paper_out[pl.ds(q * tile_rows, tile_rows), :] = classes * updated
            else:
                rounded = updated.astype(BF16).astype(F32)
                labels[q] = rounded
                gap = jnp.zeros((code.shape[1] - tile_rows, classes), F32)
                labels_t[q] = jnp.concatenate([rounded, gap], axis=0).T.astype(BF16)

    drain(weights.at[pl.ds(1, NX - 1)], w_send)
    for r in range(ROUNDS):
        rows = SEED_CLASSES if r == 0 else classes
        drain(xr.at[r, :, :, pl.ds(0, rows)], xs_send.at[r])
        drain(yr[r].at[:, :, pl.ds(0, rows)], ys_send.at[r])
        drain(yb.at[r], yb_send.at[r])
        drain(xa.at[r, :, pl.ds(1, NX - 1)], xa_send.at[r])

    def sent(k, carry):
        drain(got1.at[k], ss1.at[k])
        drain(got2.at[k], ss2.at[k])
        return carry

    lax.fori_loop(0, ROUNDS * 2 * ITERS, sent, 0)


def on_device(
    tile_values, tile_paper, tile_author, tile_count, seed_class, train_mask, class_prior, class_target
):
    slots, tile_rows, tile_cols = tile_values.shape
    classes = class_prior.shape[0]
    padded = -(-tile_rows // 128) * 128
    code = jnp.where(train_mask == 1, seed_class, -1).reshape(2, tile_rows)
    code = jnp.pad(code, ((0, 0), (0, padded - tile_rows)), constant_values=-1)
    smem, vmem = pl.BlockSpec(memory_space=pltpu.SMEM), pl.BlockSpec(memory_space=pltpu.VMEM)
    dma = pltpu.SemaphoreType.DMA
    sums = ROUNDS * 2 * ITERS
    tall, wide = (classes, tile_cols), (tile_cols, classes)
    return pl.pallas_call(
        kernel,
        out_shape=(
            jax.ShapeDtypeStruct((2 * tile_rows, classes), F32),
            jax.ShapeDtypeStruct((2 * tile_cols, classes), F32),
        ),
        in_specs=[pl.BlockSpec(memory_space=pl.ANY), smem, smem, smem, vmem, vmem, vmem],
        out_specs=(vmem, vmem),
        scratch_shapes=[
            pltpu.VMEM((slots, tile_rows, tile_cols), BF16),
            pltpu.VMEM((2, NY, tile_rows, NX * tile_cols), BF16),
            pltpu.VMEM((2, classes, padded), BF16),
            pltpu.VMEM((2, tile_rows, classes), F32),
            pltpu.VMEM((2, tile_rows, classes), F32),
            pltpu.VMEM((2, tile_rows, tile_cols), F32),
            pltpu.VMEM((NX, 3, slots, 1, classes), F32),
            pltpu.VMEM((2 * tile_cols, classes), F32),
            pltpu.VMEM((2, tile_rows, classes), F32),
            pltpu.VMEM((ROUNDS, NY, NX, *tall), BF16),
            pltpu.VMEM((ROUNDS, NY, NX - 1, *tall), BF16),
            pltpu.VMEM((NY, 2, *tall), BF16),
            pltpu.VMEM((NY - 1, 2, *tall), BF16),
            pltpu.VMEM((NY, 2, *tall), F32),
            pltpu.VMEM((NY - 1, 2, *tall), F32),
            pltpu.VMEM((ROUNDS, 2, *wide), BF16),
            pltpu.VMEM((ROUNDS, NY - 1, 2, *wide), BF16),
            pltpu.VMEM((ROUNDS, NY, NX - 1, *wide), BF16),
            pltpu.VMEM((ROUNDS, NY, NX, *wide), BF16),
            pltpu.VMEM((sums, 1, classes), F32),
            pltpu.VMEM((sums, len(ZC), 1, classes), F32),
            pltpu.VMEM((sums, 1, classes), F32),
            pltpu.VMEM((sums, len(YX), 1, classes), F32),
            dma(()), dma(()), dma(()),
            dma((ROUNDS, NY)), dma((ROUNDS,)), dma((ROUNDS,)), dma((ROUNDS,)),
            dma((ROUNDS, NY - 1)), dma((ROUNDS,)), dma((ROUNDS, NY)), dma((ROUNDS,)),
            dma((sums,)), dma((sums,)), dma((sums,)), dma((sums,)),
        ],
        compiler_params=pltpu.CompilerParams(
            collective_id=0, has_side_effects=True, vmem_limit_bytes=56 * 1024 * 1024
        ),
        name="propagate",
    )(
        tile_values, tile_paper, tile_author, tile_count, code,
        class_prior.reshape(1, classes), class_target.reshape(1, classes),
    )


def solution(mesh):
    placed = (
        P(("grp", "blk"), None, None),
        P(("grp", "blk")),
        P(("grp", "blk")),
        P(("grp", "blk")),
        P(("grp", "blk")),
        P(("grp", "blk")),
        P(),
        P(),
    )
    return jax.shard_map(
        on_device,
        mesh=mesh,
        in_specs=placed,
        out_specs=(P(("grp", "blk"), None), P(("grp", "blk"), None)),
        check_vma=False,
    )
```

```python
import functools
import itertools

import jax
import jax.numpy as jnp
from jax import lax
from jax.experimental import pallas as pl
from jax.experimental.pallas import tpu as pltpu
from jax.sharding import PartitionSpec as P

ITERS = 4
ROUNDS = 2
SEED_CLASSES = 160
KEEP = 0.8
MESH = pl.DeviceIdType.MESH
NX, NY, NZ, NC = 4, 8, 8, 2
F32, BF16 = jnp.float32, jnp.bfloat16


def add(terms):
    return functools.reduce(lambda a, b: a + b, terms)


def by_distance(sizes):
    offsets = [o for o in itertools.product(*map(range, sizes)) if any(o)]
    return sorted(offsets, key=lambda o: -sum(min(k, n - k) for k, n in zip(o, sizes)))


YX = by_distance((NY, NX))
ZC = by_distance((NZ, NC))


def kernel(
    tiles_hbm, pick_paper, pick_author, count, code, prior_ref, target_ref,
    paper_out, author_out,
    tiles, masked, labels_t, seeds, labels, degree, weights, author_k, paper_k,
    px, xr, yout, yin, own, yb, xs, xa,
    sum1, got1, sum2, got2,
    tile_sem, w_send, w_recv, xr_sem, xs_send, yin_sem, yout_send, yb_sem, yb_send, xa_sem, xa_send,
    ss1, rs1, ss2, rs2,
):
    slots, tile_rows, tile_cols = tiles_hbm.shape
    classes = prior_ref.shape[1]
    g, b = lax.axis_index("grp"), lax.axis_index("blk")
    z, c, y, x = lax.div(g, NC), lax.rem(g, NC), lax.div(b, NX), lax.rem(b, NX)

    def at(dy=0, dx=0):
        return (g, lax.rem(y + dy, NY) * NX + lax.rem(x + dx, NX))

    def across(dz, dc):
        return (lax.rem(z + dz, NZ) * NC + lax.rem(c + dc, NC), b)

    def send(src, dst, send_sem, recv_sem, device):
        pltpu.make_async_remote_copy(
            src_ref=src, dst_ref=dst, send_sem=send_sem, recv_sem=recv_sem,
            device_id=device, device_id_type=MESH,
        ).start()

    def drain(ref, sem):
        pltpu.make_async_copy(ref, ref, sem).wait()

    def sum_start(k, row):
        sum1[k] = row
        for j, (dz, dc) in enumerate(ZC):
            send(sum1.at[k], got1.at[k, j], ss1.at[k], rs1.at[k], across(dz, dc))

    def sum_middle(k):
        drain(got1.at[k], rs1.at[k])
        sum2[k] = sum1[k] + jnp.sum(got1[k], axis=0)
        for j, (dy, dx) in enumerate(YX):
            send(sum2.at[k], got2.at[k, j], ss2.at[k], rs2.at[k], at(dy, dx))

    def sum_end(k):
        drain(got2.at[k], rs2.at[k])
        return target_ref[...] / (sum2[k] + jnp.sum(got2[k], axis=0))

    load = pltpu.make_async_copy(tiles_hbm, tiles, tile_sem)
    load.start()
    barrier = pltpu.get_barrier_semaphore()
    for dy, dx in YX:
        pl.semaphore_signal(barrier, inc=1, device_id=at(dy, dx), device_id_type=MESH)
    for dz, dc in ZC:
        pl.semaphore_signal(barrier, inc=1, device_id=across(dz, dc), device_id_type=MESH)

    def slot_weights(s, carry):
        live = jnp.where(s < count[0], 1.0, 0.0)
        second = jnp.where(pick_author[s] == 1, 1.0, 0.0)
        for t, value in enumerate(((1.0 - second) * live, second * live, second)):
            weights[0, t, s] = jnp.full((1, classes), value, F32)
        return carry

    lax.fori_loop(0, slots, slot_weights, 0)
    for q in range(2):
        row = lax.broadcasted_iota(jnp.int32, (classes, code.shape[1]), 0)
        hot = jnp.where(row == code[pl.ds(q, 1), :], 1.0, 0.0)
        labels_t[q] = hot.astype(BF16)
        seeds[q] = hot.T[:tile_rows]
        labels[q] = seeds[q]
    pl.semaphore_wait(barrier, len(YX) + len(ZC))
    for dx in range(1, NX):
        send(weights.at[0], weights.at[dx], w_send, w_recv, at(0, dx))
    load.wait()

    def far_first(i):
        half = lax.div(i + 1, 2)
        return 4 + half - 2 * half * lax.rem(i, 2)

    def slot_of(oy, dx):
        return lax.rem(y + oy, NY) * NX + lax.rem(x + dx, NX)

    def forward(r, rows, between, middle, last):
        def parcels(i, carry):
            oy = far_first(i)
            for dx in (2, 1, 3, 0):
                s = slot_of(oy, dx)
                value = jnp.dot(
                    labels_t[pick_paper[s], :rows, :tile_rows], tiles[s], preferred_element_type=F32
                )
                px[r, oy, dx, :rows] = value.astype(BF16)
                if dx:
                    send(
                        px.at[r, oy, dx, pl.ds(0, rows)], xr.at[r, oy, dx - 1, pl.ds(0, rows)],
                        xs_send.at[r], xr_sem.at[r, oy], at(0, dx),
                    )
            return carry

        lax.fori_loop(0, NY, parcels, 0)
        if r == 0:
            drain(weights.at[pl.ds(1, NX - 1)], w_recv)

        def row_sum(oy, t, span):
            s = slot_of(oy, 0)
            parts = [px[r, oy, 0, span]] + [xr[r, oy, dx - 1, span] for dx in range(1, NX)]
            return add(part.astype(F32) * weights[dx, t, s][:, :tile_cols] for dx, part in enumerate(parts))

        half = rows // 2

        def hop(step):
            for part in range(2):
                span = pl.ds(part * half, half)
                for way in range(2):
                    away = NY // 2 - step
                    oy = away if way == 0 else NY - away
                    if step == 0:
                        chosen = [way]
                    else:
                        chosen = [0, 1]
                        before = [way] if step == 1 else [0, 1]
                        drain(yin.at[r, way, step - 1, pl.ds(before[0], len(before)), span], yin_sem.at[r, way, step - 1, part])
                    if part == 0 and (step > 0 or way == 0):
                        drain(xr.at[r, oy, :, pl.ds(0, rows)], xr_sem.at[r, oy])
                    for t in chosen:
                        total = row_sum(oy, t, span)
                        if step > 0 and t in before:
                            total = total + yin[r, way, step - 1, t, span]
                        yout[r, way, step, t, span] = total
                    tiles_sent = pl.ds(chosen[0], len(chosen))
                    send(
                        yout.at[r, way, step, tiles_sent, span], yin.at[r, way, step, tiles_sent, span],
                        yout_send.at[r, way, step], yin_sem.at[r, way, step, part], at(1 if way == 0 else NY - 1, 0),
                    )

        hop(0)
        between()
        hop(1)
        middle()
        hop(2)
        hop(3)
        drain(xr.at[r, 0, :, pl.ds(0, rows)], xr_sem.at[r, 0])
        totals = [row_sum(0, t, pl.ds(0, rows)) for t in range(2)]
        first = last()
        for way in range(2):
            for part in range(2):
                drain(yin.at[r, way, NY // 2 - 1, :, pl.ds(part * half, half)], yin_sem.at[r, way, NY // 2 - 1, part])
        for t, total in enumerate(totals):
            for way in range(2):
                total = total + yin[r, way, NY // 2 - 1, t, :rows]
            if rows < classes:
                total = jnp.concatenate([total, jnp.zeros((classes - rows, tile_cols), F32)], axis=0)
            k = total.T + prior_ref[...]
            author_k[pl.ds(t * tile_cols, tile_cols), :] = k
            own[r, t] = k.astype(BF16)
        return first

    def mask_tiles():
        degree[...] = jnp.zeros_like(degree)

        def row(oy, carry):
            for dx in range(NX):
                s = slot_of(oy, (NX - dx) % NX)
                live = jnp.where(s < count[0], 1.0, 0.0)
                for q in range(2):
                    keep = jnp.where(pick_paper[s] == q, live, 0.0)
                    part = tiles[s] * jnp.full((1, tile_cols), keep, F32).astype(BF16)
                    masked[q, oy, :, dx * tile_cols:(dx + 1) * tile_cols] = part
                    degree[q] += part.astype(F32)
            return carry

        lax.fori_loop(0, NY, row, 0)

    def first_author_sum():
        nodes = 2.0 * tile_cols
        sums = [
            jnp.sum(jnp.sum(degree[q], axis=1, keepdims=True) * labels[q], axis=0, keepdims=True) for q in range(2)
        ]
        return sums[0] + sums[1] + nodes * prior_ref[...]

    def pass_on(r, away):
        for way in range(2):
            here = own.at[r] if away == 1 else yb.at[r, (NY - away if way == 0 else away - 2)]
            there = yb.at[r, (NY - away - 1 if way == 0 else away - 1)]
            if away == NY // 2:
                here, there = here.at[pl.ds(way, 1)], there.at[pl.ds(way, 1)]
            oy = NY - away if way == 0 else away
            send(here, there, yb_send.at[r, way, away - 1], yb_sem.at[r, oy - 1], at(1 if way == 0 else NY - 1, 0))

    def spread(r, oy, both):
        s = slot_of(oy, 0)
        for dx in (2, 1, 3, 0):
            second = weights[(NX - dx) % NX, 2, s] > 0.5
            chosen = jnp.where(second, both[1].astype(F32), both[0].astype(F32))
            if dx:
                xs[r, oy, dx - 1] = chosen.astype(BF16)
                send(xs.at[r, oy, dx - 1], xa.at[r, oy, dx], xa_send.at[r], xa_sem.at[r, oy], at(0, dx))
            else:
                xa[r, oy, 0] = chosen.astype(BF16)

    def spread_from(r, away):
        for oy in (NY - away, away)[: 1 if away == NY // 2 else 2]:
            drain(yb.at[r, oy - 1], yb_sem.at[r, oy - 1])
        if away < NY // 2:
            pass_on(r, away + 1)
        for oy in (NY - away, away)[: 1 if away == NY // 2 else 2]:
            spread(r, oy, [yb[r, oy - 1, 0], yb[r, oy - 1, 1]])

    def paper_masses(r, columns):
        for q in range(2):
            paper_k[q] = jnp.broadcast_to(prior_ref[...], (tile_rows, classes))

        def step(i, carry):
            oy = far_first(NY - 1 - i)
            drain(xa.at[r, oy, pl.ds(1, NX - 1)], xa_sem.at[r, oy])
            scaled = xa[r, oy].astype(F32).reshape(NX * tile_cols, classes) * columns
            share = (scaled * (1.0 / jnp.sum(scaled, axis=1, keepdims=True))).astype(BF16)
            for q in range(2):
                paper_k[q] += jnp.dot(masked[q, oy], share, preferred_element_type=F32)
            return carry

        lax.fori_loop(0, NY, step, 0)

    def sum_all(k, row):
        sum_start(k, row)
        sum_middle(k)
        return sum_end(k)

    def rows_of(k, columns):
        return 1.0 / jnp.sum(k * columns, axis=1, keepdims=True)

    for r in range(ROUNDS):
        base = r * 2 * ITERS
        final = r == ROUNDS - 1

        def between():
            if r == 0:
                mask_tiles()
            sum_start(base, first_author_sum())

        columns = forward(
            r, SEED_CLASSES if r == 0 else classes, between, lambda: sum_middle(base), lambda: sum_end(base)
        )
        pass_on(r, 1)
        for i in range(1, ITERS):
            k = author_k[...]
            sum_start(base + i, jnp.sum(k * rows_of(k, columns), axis=0, keepdims=True))
            if i == 1:
                spread(r, 0, [own[r, 0], own[r, 1]])
            else:
                spread_from(r, 2 * i - 2)
            sum_middle(base + i)
            if i < ITERS - 1:
                spread_from(r, 2 * i - 1)
            columns = sum_end(base + i)
        if final:
            k = author_k[...]
            author_out[...] = classes * (rows_of(k, columns) * k * columns)
        paper_masses(r, columns)
        columns = sum_all(base + ITERS, add(jnp.sum(paper_k[q], axis=0, keepdims=True) for q in range(2)))

        def iterate(i, columns):
            row = add(
                jnp.sum(paper_k[q] * rows_of(paper_k[q], columns), axis=0, keepdims=True) for q in range(2)
            )
            return sum_all(base + ITERS + i, row)

        columns = lax.fori_loop(1, ITERS, iterate, columns)
        for q in range(2):
            k = paper_k[q]
            updated = KEEP * (rows_of(k, columns) * k * columns) + (1.0 - KEEP) * seeds[q]
            if final:
                paper_out[pl.ds(q * tile_rows, tile_rows), :] = classes * updated
            else:
                rounded = updated.astype(BF16).astype(F32)
                labels[q] = rounded
                gap = jnp.zeros((code.shape[1] - tile_rows, classes), F32)
                labels_t[q] = jnp.concatenate([rounded, gap], axis=0).T.astype(BF16)

    drain(weights.at[pl.ds(1, NX - 1)], w_send)
    for r in range(ROUNDS):
        rows = SEED_CLASSES if r == 0 else classes
        drain(xr.at[r, :, :, pl.ds(0, rows)], xs_send.at[r])
        for way in range(2):
            for step in range(NY // 2):
                sent_tiles = pl.ds(way, 1) if step == 0 else pl.ds(0, 2)
                drain(yout.at[r, way, step, sent_tiles, pl.ds(0, rows)], yout_send.at[r, way, step])
                last_hop = step == NY // 2 - 1
                drain(yb.at[r, 0, pl.ds(0, 1 if last_hop else 2)], yb_send.at[r, way, step])
        drain(xa.at[r, :, pl.ds(1, NX - 1)], xa_send.at[r])

    def sent(k, carry):
        drain(got1.at[k], ss1.at[k])
        drain(got2.at[k], ss2.at[k])
        return carry

    lax.fori_loop(0, ROUNDS * 2 * ITERS, sent, 0)


def on_device(
    tile_values, tile_paper, tile_author, tile_count, seed_class, train_mask, class_prior, class_target
):
    slots, tile_rows, tile_cols = tile_values.shape
    classes = class_prior.shape[0]
    padded = -(-tile_rows // 128) * 128
    code = jnp.where(train_mask == 1, seed_class, -1).reshape(2, tile_rows)
    code = jnp.pad(code, ((0, 0), (0, padded - tile_rows)), constant_values=-1)
    smem, vmem = pl.BlockSpec(memory_space=pltpu.SMEM), pl.BlockSpec(memory_space=pltpu.VMEM)
    dma = pltpu.SemaphoreType.DMA
    sums = ROUNDS * 2 * ITERS
    tall, wide = (classes, tile_cols), (tile_cols, classes)
    return pl.pallas_call(
        kernel,
        out_shape=(
            jax.ShapeDtypeStruct((2 * tile_rows, classes), F32),
            jax.ShapeDtypeStruct((2 * tile_cols, classes), F32),
        ),
        in_specs=[pl.BlockSpec(memory_space=pl.ANY), smem, smem, smem, vmem, vmem, vmem],
        out_specs=(vmem, vmem),
        scratch_shapes=[
            pltpu.VMEM((slots, tile_rows, tile_cols), BF16),
            pltpu.VMEM((2, NY, tile_rows, NX * tile_cols), BF16),
            pltpu.VMEM((2, classes, padded), BF16),
            pltpu.VMEM((2, tile_rows, classes), F32),
            pltpu.VMEM((2, tile_rows, classes), F32),
            pltpu.VMEM((2, tile_rows, tile_cols), F32),
            pltpu.VMEM((NX, 3, slots, 1, classes), F32),
            pltpu.VMEM((2 * tile_cols, classes), F32),
            pltpu.VMEM((2, tile_rows, classes), F32),
            pltpu.VMEM((ROUNDS, NY, NX, *tall), BF16),
            pltpu.VMEM((ROUNDS, NY, NX - 1, *tall), BF16),
            pltpu.VMEM((ROUNDS, 2, NY // 2, 2, *tall), F32),
            pltpu.VMEM((ROUNDS, 2, NY // 2, 2, *tall), F32),
            pltpu.VMEM((ROUNDS, 2, *wide), BF16),
            pltpu.VMEM((ROUNDS, NY - 1, 2, *wide), BF16),
            pltpu.VMEM((ROUNDS, NY, NX - 1, *wide), BF16),
            pltpu.VMEM((ROUNDS, NY, NX, *wide), BF16),
            pltpu.VMEM((sums, 1, classes), F32),
            pltpu.VMEM((sums, len(ZC), 1, classes), F32),
            pltpu.VMEM((sums, 1, classes), F32),
            pltpu.VMEM((sums, len(YX), 1, classes), F32),
            dma(()), dma(()), dma(()),
            dma((ROUNDS, NY)), dma((ROUNDS,)), dma((ROUNDS, 2, NY // 2, 2)), dma((ROUNDS, 2, NY // 2)),
            dma((ROUNDS, NY - 1)), dma((ROUNDS, 2, NY // 2)), dma((ROUNDS, NY)), dma((ROUNDS,)),
            dma((sums,)), dma((sums,)), dma((sums,)), dma((sums,)),
        ],
        compiler_params=pltpu.CompilerParams(
            collective_id=0, has_side_effects=True, vmem_limit_bytes=56 * 1024 * 1024
        ),
        name="propagate",
    )(
        tile_values, tile_paper, tile_author, tile_count, code,
        class_prior.reshape(1, classes), class_target.reshape(1, classes),
    )


def solution(mesh):
    placed = (
        P(("grp", "blk"), None, None),
        P(("grp", "blk")),
        P(("grp", "blk")),
        P(("grp", "blk")),
        P(("grp", "blk")),
        P(("grp", "blk")),
        P(),
        P(),
    )
    return jax.shard_map(
        on_device,
        mesh=mesh,
        in_specs=placed,
        out_specs=(P(("grp", "blk"), None), P(("grp", "blk"), None)),
        check_vma=False,
    )
```

```python
import functools
import itertools

import jax
import jax.numpy as jnp
from jax import lax
from jax.experimental import pallas as pl
from jax.experimental.pallas import tpu as pltpu
from jax.sharding import PartitionSpec as P

ITERS = 4
ROUNDS = 2
SEED_CLASSES = 153
SEED_ROWS = 160
KEEP = 0.8
MESH = pl.DeviceIdType.MESH
NX, NY, NZ, NC = 4, 8, 8, 2
F32, BF16 = jnp.float32, jnp.bfloat16


def add(terms):
    return functools.reduce(lambda a, b: a + b, terms)


def by_distance(sizes):
    offsets = [o for o in itertools.product(*map(range, sizes)) if any(o)]
    return sorted(offsets, key=lambda o: -sum(min(k, n - k) for k, n in zip(o, sizes)))


YX = by_distance((NY, NX))
ZC = by_distance((NZ, NC))


def kernel(
    tiles_hbm, pick_paper, pick_author, count, seed_class, train_mask, prior_ref, target_ref,
    paper_out, author_out,
    tiles, masked, code, labels_t, seeds, tally, weights, degree, author_k, paper_k,
    px, xr, yout, yin, own, yb, xs, xa,
    sum1, got1, sum2, got2,
    tile_sem, w_send, w_recv, xr_sem, xs_send, yin_sem, yout_send, yb_sem, yb_send, xa_sem, xa_send,
    ss1, rs1, ss2, rs2,
):
    slots, tile_rows, tile_cols = tiles_hbm.shape
    classes = prior_ref.shape[1]
    g, b = lax.axis_index("grp"), lax.axis_index("blk")
    z, c, y, x = lax.div(g, NC), lax.rem(g, NC), lax.div(b, NX), lax.rem(b, NX)

    def at(dy=0, dx=0):
        return (g, lax.rem(y + dy, NY) * NX + lax.rem(x + dx, NX))

    def across(dz, dc):
        return (lax.rem(z + dz, NZ) * NC + lax.rem(c + dc, NC), b)

    def send(src, dst, send_sem, recv_sem, device):
        pltpu.make_async_remote_copy(
            src_ref=src, dst_ref=dst, send_sem=send_sem, recv_sem=recv_sem,
            device_id=device, device_id_type=MESH,
        ).start()

    def drain(ref, sem):
        pltpu.make_async_copy(ref, ref, sem).wait()

    def sum_start(k, row):
        sum1[k] = row
        for j, (dz, dc) in enumerate(ZC):
            send(sum1.at[k], got1.at[k, j], ss1.at[k], rs1.at[k], across(dz, dc))

    def sum_middle(k):
        drain(got1.at[k], rs1.at[k])
        sum2[k] = sum1[k] + jnp.sum(got1[k], axis=0)
        for j, (dy, dx) in enumerate(YX):
            send(sum2.at[k], got2.at[k, j], ss2.at[k], rs2.at[k], at(dy, dx))

    def sum_end(k):
        drain(got2.at[k], rs2.at[k])
        return target_ref[...] / (sum2[k] + jnp.sum(got2[k], axis=0))

    load = pltpu.make_async_copy(tiles_hbm, tiles, tile_sem)
    load.start()
    barrier = pltpu.get_barrier_semaphore()
    for dy, dx in YX:
        pl.semaphore_signal(barrier, inc=1, device_id=at(dy, dx), device_id_type=MESH)
    for dz, dc in ZC:
        pl.semaphore_signal(barrier, inc=1, device_id=across(dz, dc), device_id_type=MESH)

    def slot_weights(s, carry):
        live = jnp.where(s < count[0], 1.0, 0.0)
        second = jnp.where(pick_author[s] == 1, 1.0, 0.0)
        for t, value in enumerate(((1.0 - second) * live, second * live, second)):
            weights[0, t, s] = jnp.full((1, classes), value, F32)
        return carry

    lax.fori_loop(0, slots, slot_weights, 0)
    code[...] = jnp.full(code.shape, -1, jnp.int32)
    code[:, :tile_rows] = jnp.where(train_mask[...] == 1, seed_class[...], -1)

    def one_hot(q):
        row = lax.broadcasted_iota(jnp.int32, (classes, code.shape[1]), 0)
        return jnp.where(row == code[pl.ds(q, 1), :], 1.0, 0.0)

    for q in range(2):
        row = lax.broadcasted_iota(jnp.int32, labels_t.shape[1:], 0)
        extra = (row == SEED_CLASSES) | (row == SEED_CLASSES + 1)
        labels_t[q] = jnp.where(extra, 1.0, one_hot(q)).astype(BF16)
    pl.semaphore_wait(barrier, len(YX) + len(ZC))
    for dx in range(1, NX):
        send(weights.at[0], weights.at[dx], w_send, w_recv, at(0, dx))
    load.wait()

    def far_first(i):
        half = lax.div(i + 1, 2)
        return 4 + half - 2 * half * lax.rem(i, 2)

    def slot_of(oy, dx):
        return lax.rem(y + oy, NY) * NX + lax.rem(x + dx, NX)

    def forward(r, rows, begin, middle, last):
        tally[...] = jnp.zeros_like(tally)

        def parcels(i, carry):
            oy = far_first(i)
            for dx in (2, 1, 3, 0):
                s = slot_of(oy, dx)
                value = jnp.dot(
                    labels_t[pick_paper[s], :rows, :tile_rows], tiles[s], preferred_element_type=F32
                )
                if r == 0:
                    row = lax.broadcasted_iota(jnp.int32, value.shape, 0)
                    low = value - value.astype(BF16).astype(F32)
                    value = jnp.where(row == SEED_CLASSES + 1, low, value)
                parcel = value.astype(BF16)
                px[r, oy, dx, :rows] = parcel
                tally[:rows, :] += parcel.astype(F32) * jnp.where(s < count[0], 1.0, 0.0)
                if dx:
                    send(
                        px.at[r, oy, dx, pl.ds(0, rows)], xr.at[r, oy, dx - 1, pl.ds(0, rows)],
                        xs_send.at[r], xr_sem.at[r, oy], at(0, dx),
                    )
            return carry

        lax.fori_loop(0, NY, parcels, 0)
        begin()

        def row_sum(oy, t, span):
            s = slot_of(oy, 0)
            parts = [px[r, oy, 0, span]] + [xr[r, oy, dx - 1, span] for dx in range(1, NX)]
            return add(part.astype(F32) * weights[dx, t, s][:, :tile_cols] for dx, part in enumerate(parts))

        size = 64 if rows % 64 == 0 else 32
        parts = rows // size

        def hop(step):
            for part in range(parts):
                span = pl.ds(part * size, size)
                for way in range(2):
                    away = NY // 2 - step
                    oy = away if way == 0 else NY - away
                    if step == 0:
                        chosen = [way]
                    else:
                        chosen = [0, 1]
                        before = [way] if step == 1 else [0, 1]
                        drain(yin.at[r, way, step - 1, pl.ds(before[0], len(before)), span], yin_sem.at[r, way, step - 1, part])
                    if part == 0 and (step > 0 or way == 0):
                        drain(xr.at[r, oy, :, pl.ds(0, rows)], xr_sem.at[r, oy])
                    for t in chosen:
                        total = row_sum(oy, t, span)
                        if step > 0 and t in before:
                            total = total + yin[r, way, step - 1, t, span]
                        yout[r, way, step, t, span] = total
                    tiles_sent = pl.ds(chosen[0], len(chosen))
                    send(
                        yout.at[r, way, step, tiles_sent, span], yin.at[r, way, step, tiles_sent, span],
                        yout_send.at[r, way, step], yin_sem.at[r, way, step, part], at(1 if way == 0 else NY - 1, 0),
                    )

        hop(0)
        hop(1)
        middle()
        hop(2)
        hop(3)
        drain(xr.at[r, 0, :, pl.ds(0, rows)], xr_sem.at[r, 0])
        totals = [row_sum(0, t, pl.ds(0, rows)) for t in range(2)]
        first = last()
        for way in range(2):
            for part in range(parts):
                drain(yin.at[r, way, NY // 2 - 1, :, pl.ds(part * size, size)], yin_sem.at[r, way, NY // 2 - 1, part])
        for t, total in enumerate(totals):
            for way in range(2):
                total = total + yin[r, way, NY // 2 - 1, t, :rows]
            if r == 0:
                total = jnp.concatenate([total, jnp.zeros((classes - rows, tile_cols), F32)], axis=0)
            mass = total.T
            if r == 0:
                column = lax.broadcasted_iota(jnp.int32, mass.shape, 1)
                degree[pl.ds(t * tile_cols, tile_cols), :] = jnp.sum(
                    jnp.where(column >= SEED_CLASSES, mass, 0.0), axis=1, keepdims=True
                )
                mass = jnp.where(column >= SEED_CLASSES, 0.0, mass)
            k = mass + prior_ref[...]
            author_k[pl.ds(t * tile_cols, tile_cols), :] = k
            own[r, t] = k.astype(BF16)
        return first

    def mask_tiles():
        def row(oy, carry):
            for dx in range(NX):
                s = slot_of(oy, (NX - dx) % NX)
                live = jnp.where(s < count[0], 1.0, 0.0)
                for q in range(2):
                    keep = jnp.where(pick_paper[s] == q, live, 0.0)
                    keep = jnp.full((1, tile_cols), keep, F32).astype(BF16)
                    masked[q, oy, :, dx * tile_cols:(dx + 1) * tile_cols] = tiles[s] * keep
            return carry

        lax.fori_loop(0, NY, row, 0)

    def keep_seeds():
        for q in range(2):
            seeds[q] = one_hot(q).T[:tile_rows]

    def first_author_sum(r):
        mass = jnp.sum(tally[...].T, axis=0, keepdims=True)
        if r == 0:
            mass = jnp.where(lax.broadcasted_iota(jnp.int32, mass.shape, 1) >= SEED_CLASSES, 0.0, mass)
        return mass + 2.0 * tile_cols * prior_ref[...]

    def first_paper_sum(columns):
        k = author_k[...]
        share = rows_of(k, columns) * k * columns
        if final:
            author_out[...] = share
        return jnp.sum(degree[...] * share, axis=0, keepdims=True) + 2.0 * tile_rows * prior_ref[...]

    def pass_on(r, away):
        for way in range(2):
            here = own.at[r] if away == 1 else yb.at[r, (NY - away if way == 0 else away - 2)]
            there = yb.at[r, (NY - away - 1 if way == 0 else away - 1)]
            if away == NY // 2:
                here, there = here.at[pl.ds(way, 1)], there.at[pl.ds(way, 1)]
            oy = NY - away if way == 0 else away
            send(here, there, yb_send.at[r, way, away - 1], yb_sem.at[r, oy - 1], at(1 if way == 0 else NY - 1, 0))

    def spread(r, oy, both):
        s = slot_of(oy, 0)
        for dx in (2, 1, 3, 0):
            second = weights[(NX - dx) % NX, 2, s] > 0.5
            chosen = jnp.where(second, both[1].astype(F32), both[0].astype(F32))
            if dx:
                xs[r, oy, dx - 1] = chosen.astype(BF16)
                send(xs.at[r, oy, dx - 1], xa.at[r, oy, dx], xa_send.at[r], xa_sem.at[r, oy], at(0, dx))
            else:
                xa[r, oy, 0] = chosen.astype(BF16)

    def spread_from(r, away):
        for oy in (NY - away, away)[: 1 if away == NY // 2 else 2]:
            drain(yb.at[r, oy - 1], yb_sem.at[r, oy - 1])
        if away < NY // 2:
            pass_on(r, away + 1)
        for oy in (NY - away, away)[: 1 if away == NY // 2 else 2]:
            spread(r, oy, [yb[r, oy - 1, 0], yb[r, oy - 1, 1]])

    def paper_masses(r, columns, first, stop):
        def step(i, carry):
            oy = far_first(NY - 1 - i)
            drain(xa.at[r, oy, pl.ds(1, NX - 1)], xa_sem.at[r, oy])
            scaled = xa[r, oy].astype(F32).reshape(NX * tile_cols, classes) * columns
            share = (scaled * (1.0 / jnp.sum(scaled, axis=1, keepdims=True))).astype(BF16)
            for q in range(2):
                paper_k[q] += jnp.dot(masked[q, oy], share, preferred_element_type=F32)
            return carry

        lax.fori_loop(first, stop, step, 0)

    def sum_all(k, row):
        sum_start(k, row)
        sum_middle(k)
        return sum_end(k)

    def rows_of(k, columns):
        return 1.0 / jnp.sum(k * columns, axis=1, keepdims=True)

    def weighted_sum(blocks, columns):
        total = jnp.zeros((8, classes), F32)
        for block in blocks:
            k = block[...]
            total = total + jnp.sum((k * rows_of(k, columns)).reshape(-1, 8, classes), axis=0)
        return jnp.sum(total, axis=0, keepdims=True)

    author_blocks = [author_k.at[pl.ds(i, 64)] for i in range(0, 2 * tile_cols, 64)]
    paper_blocks = [paper_k.at[q, pl.ds(i, 64)] for q in range(2) for i in range(0, tile_rows, 64)]

    for r in range(ROUNDS):
        base = r * 2 * ITERS
        final = r == ROUNDS - 1

        def begin():
            sum_start(base, first_author_sum(r))
            if r == 0:
                drain(weights.at[pl.ds(1, NX - 1)], w_recv)

        columns = forward(
            r, SEED_ROWS if r == 0 else classes, begin, lambda: sum_middle(base), lambda: sum_end(base)
        )
        pass_on(r, 1)
        for i in range(1, ITERS):
            sum_start(base + i, weighted_sum(author_blocks, columns))
            if i == 1:
                spread(r, 0, [own[r, 0], own[r, 1]])
                if r == 0:
                    mask_tiles()
            else:
                spread_from(r, 2 * i - 2)
            sum_middle(base + i)
            if i < ITERS - 1:
                spread_from(r, 2 * i - 1)
            elif r == 0:
                keep_seeds()
            columns = sum_end(base + i)
        sum_start(base + ITERS, first_paper_sum(columns))
        for q in range(2):
            paper_k[q] = jnp.broadcast_to(prior_ref[...], (tile_rows, classes))
        paper_masses(r, columns, 0, NY // 2)
        sum_middle(base + ITERS)
        paper_masses(r, columns, NY // 2, NY)
        columns = sum_end(base + ITERS)

        def iterate(i, columns):
            return sum_all(base + ITERS + i, weighted_sum(paper_blocks, columns))

        columns = lax.fori_loop(1, ITERS, iterate, columns)
        for q in range(2):
            k = paper_k[q]
            updated = KEEP * (rows_of(k, columns) * k * columns) + (1.0 - KEEP) * seeds[q]
            if final:
                paper_out[pl.ds(q * tile_rows, tile_rows), :] = updated
            else:
                rounded = updated.astype(BF16).astype(F32)
                gap = jnp.zeros((code.shape[1] - tile_rows, classes), F32)
                labels_t[q] = jnp.concatenate([rounded, gap], axis=0).T.astype(BF16)

    drain(weights.at[pl.ds(1, NX - 1)], w_send)
    for r in range(ROUNDS):
        rows = SEED_ROWS if r == 0 else classes
        drain(xr.at[r, :, :, pl.ds(0, rows)], xs_send.at[r])
        for way in range(2):
            for step in range(NY // 2):
                sent_tiles = pl.ds(way, 1) if step == 0 else pl.ds(0, 2)
                drain(yout.at[r, way, step, sent_tiles, pl.ds(0, rows)], yout_send.at[r, way, step])
                last_hop = step == NY // 2 - 1
                drain(yb.at[r, 0, pl.ds(0, 1 if last_hop else 2)], yb_send.at[r, way, step])
        drain(xa.at[r, :, pl.ds(1, NX - 1)], xa_send.at[r])

    def sent(k, carry):
        drain(got1.at[k], ss1.at[k])
        drain(got2.at[k], ss2.at[k])
        return carry

    lax.fori_loop(0, ROUNDS * 2 * ITERS, sent, 0)


def scores(updated, share, paper_scores, author_scores):
    paper_scores[...] = updated.shape[1] * updated[...]
    author_scores[...] = share.shape[1] * share[...]


def on_device(
    tile_values, tile_paper, tile_author, tile_count, seed_class, train_mask, class_prior, class_target
):
    slots, tile_rows, tile_cols = tile_values.shape
    classes = class_prior.shape[0]
    padded = -(-tile_rows // 128) * 128
    smem, vmem = pl.BlockSpec(memory_space=pltpu.SMEM), pl.BlockSpec(memory_space=pltpu.VMEM)
    dma = pltpu.SemaphoreType.DMA
    sums = ROUNDS * 2 * ITERS
    tall, wide = (classes, tile_cols), (tile_cols, classes)
    updated, share = pl.pallas_call(
        kernel,
        out_shape=(
            jax.ShapeDtypeStruct((2 * tile_rows, classes), F32),
            jax.ShapeDtypeStruct((2 * tile_cols, classes), F32),
        ),
        in_specs=[pl.BlockSpec(memory_space=pl.ANY), smem, smem, smem, vmem, vmem, vmem, vmem],
        out_specs=(vmem, vmem),
        scratch_shapes=[
            pltpu.VMEM((slots, tile_rows, tile_cols), BF16),
            pltpu.VMEM((2, NY, tile_rows, NX * tile_cols), BF16),
            pltpu.VMEM((2, padded), jnp.int32),
            pltpu.VMEM((2, classes, padded), BF16),
            pltpu.VMEM((2, tile_rows, classes), F32),
            pltpu.VMEM(tall, F32),
            pltpu.VMEM((NX, 3, slots, 1, classes), F32),
            pltpu.VMEM((2 * tile_cols, 1), F32),
            pltpu.VMEM((2 * tile_cols, classes), F32),
            pltpu.VMEM((2, tile_rows, classes), F32),
            pltpu.VMEM((ROUNDS, NY, NX, *tall), BF16),
            pltpu.VMEM((ROUNDS, NY, NX - 1, *tall), BF16),
            pltpu.VMEM((ROUNDS, 2, NY // 2, 2, *tall), F32),
            pltpu.VMEM((ROUNDS, 2, NY // 2, 2, *tall), F32),
            pltpu.VMEM((ROUNDS, 2, *wide), BF16),
            pltpu.VMEM((ROUNDS, NY - 1, 2, *wide), BF16),
            pltpu.VMEM((ROUNDS, NY, NX - 1, *wide), BF16),
            pltpu.VMEM((ROUNDS, NY, NX, *wide), BF16),
            pltpu.VMEM((sums, 1, classes), F32),
            pltpu.VMEM((sums, len(ZC), 1, classes), F32),
            pltpu.VMEM((sums, 1, classes), F32),
            pltpu.VMEM((sums, len(YX), 1, classes), F32),
            dma(()), dma(()), dma(()),
            dma((ROUNDS, NY)), dma((ROUNDS,)), dma((ROUNDS, 2, NY // 2, 8)), dma((ROUNDS, 2, NY // 2)),
            dma((ROUNDS, NY - 1)), dma((ROUNDS, 2, NY // 2)), dma((ROUNDS, NY)), dma((ROUNDS,)),
            dma((sums,)), dma((sums,)), dma((sums,)), dma((sums,)),
        ],
        compiler_params=pltpu.CompilerParams(
            collective_id=0, has_side_effects=True, vmem_limit_bytes=56 * 1024 * 1024
        ),
        name="propagate",
    )(
        tile_values, tile_paper, tile_author, tile_count,
        seed_class.reshape(2, tile_rows), train_mask.reshape(2, tile_rows),
        class_prior.reshape(1, classes), class_target.reshape(1, classes),
    )
    return pl.pallas_call(
        scores,
        out_shape=(
            jax.ShapeDtypeStruct(updated.shape, F32),
            jax.ShapeDtypeStruct(share.shape, F32),
        ),
        name="scores",
    )(updated, share)


def solution(mesh):
    placed = (
        P(("grp", "blk"), None, None),
        P(("grp", "blk")),
        P(("grp", "blk")),
        P(("grp", "blk")),
        P(("grp", "blk")),
        P(("grp", "blk")),
        P(),
        P(),
    )
    return jax.shard_map(
        on_device,
        mesh=mesh,
        in_specs=placed,
        out_specs=(P(("grp", "blk"), None), P(("grp", "blk"), None)),
        check_vma=False,
    )
```

```python
import functools
import itertools

import jax
import jax.numpy as jnp
from jax import lax
from jax.experimental import pallas as pl
from jax.experimental.pallas import tpu as pltpu
from jax.sharding import PartitionSpec as P

ITERS = 4
ROUNDS = 2
SEED_CLASSES = 153
SEED_ROWS = 160
KEEP = 0.8
MESH = pl.DeviceIdType.MESH
NX, NY, NZ, NC = 4, 8, 8, 2
F32, BF16 = jnp.float32, jnp.bfloat16


def add(terms):
    return functools.reduce(lambda a, b: a + b, terms)


def by_distance(sizes):
    offsets = [o for o in itertools.product(*map(range, sizes)) if any(o)]
    return sorted(offsets, key=lambda o: -sum(min(k, n - k) for k, n in zip(o, sizes)))


YX = by_distance((NY, NX))
ZC = by_distance((NZ, NC))


def kernel(
    tiles_hbm, pick_paper, pick_author, count, code_ref, prior_ref, target_ref,
    paper_out, author_out,
    tiles, masked, code, labels_t, seeds, tally, weights, degree, author_k, paper_k,
    px, xr, yout, yin, own, yb, xs, xa,
    sum1, got1, sum2, got2,
    tile_sem, w_send, w_recv, xr_sem, xs_send, yin_sem, yout_send, yb_sem, yb_send, xa_sem, xa_send,
    ss1, rs1, ss2, rs2,
):
    slots, tile_rows, tile_cols = tiles_hbm.shape
    classes = prior_ref.shape[1]
    g, b = lax.axis_index("grp"), lax.axis_index("blk")
    z, c, y, x = lax.div(g, NC), lax.rem(g, NC), lax.div(b, NX), lax.rem(b, NX)

    def at(dy=0, dx=0):
        return (g, lax.rem(y + dy, NY) * NX + lax.rem(x + dx, NX))

    def across(dz, dc):
        return (lax.rem(z + dz, NZ) * NC + lax.rem(c + dc, NC), b)

    def send(src, dst, send_sem, recv_sem, device):
        pltpu.make_async_remote_copy(
            src_ref=src, dst_ref=dst, send_sem=send_sem, recv_sem=recv_sem,
            device_id=device, device_id_type=MESH,
        ).start()

    def drain(ref, sem):
        pltpu.make_async_copy(ref, ref, sem).wait()

    def sum_start(k, row):
        sum1[k] = row
        for j, (dz, dc) in enumerate(ZC):
            send(sum1.at[k], got1.at[k, j], ss1.at[k], rs1.at[k], across(dz, dc))

    def sum_middle(k):
        drain(got1.at[k], rs1.at[k])
        sum2[k] = sum1[k] + jnp.sum(got1[k], axis=0)
        for j, (dy, dx) in enumerate(YX):
            send(sum2.at[k], got2.at[k, j], ss2.at[k], rs2.at[k], at(dy, dx))

    def sum_end(k):
        drain(got2.at[k], rs2.at[k])
        return target_ref[...] / (sum2[k] + jnp.sum(got2[k], axis=0))

    load = pltpu.make_async_copy(tiles_hbm, tiles, tile_sem)
    load.start()
    barrier = pltpu.get_barrier_semaphore()
    for dy, dx in YX:
        pl.semaphore_signal(barrier, inc=1, device_id=at(dy, dx), device_id_type=MESH)
    for dz, dc in ZC:
        pl.semaphore_signal(barrier, inc=1, device_id=across(dz, dc), device_id_type=MESH)

    def slot_weights(s, carry):
        live = jnp.where(s < count[0], 1.0, 0.0)
        second = jnp.where(pick_author[s] == 1, 1.0, 0.0)
        for t, value in enumerate(((1.0 - second) * live, second * live, second)):
            weights[0, t, s] = jnp.full((1, classes), value, F32)
        return carry

    lax.fori_loop(0, slots, slot_weights, 0)
    code[...] = jnp.full(code.shape, -1, jnp.int32)
    code[:, :tile_rows] = code_ref[...]

    def one_hot(q):
        row = lax.broadcasted_iota(jnp.int32, (classes, code.shape[1]), 0)
        return jnp.where(row == code[pl.ds(q, 1), :], 1.0, 0.0)

    for q in range(2):
        row = lax.broadcasted_iota(jnp.int32, labels_t.shape[1:], 0)
        extra = (row == SEED_CLASSES) | (row == SEED_CLASSES + 1)
        labels_t[q] = jnp.where(extra, 1.0, one_hot(q)).astype(BF16)
    pl.semaphore_wait(barrier, len(YX) + len(ZC))
    for dx in range(1, NX):
        send(weights.at[0], weights.at[dx], w_send, w_recv, at(0, dx))
    load.wait()

    def far_first(i):
        half = lax.div(i + 1, 2)
        return 4 + half - 2 * half * lax.rem(i, 2)

    def slot_of(oy, dx):
        return lax.rem(y + oy, NY) * NX + lax.rem(x + dx, NX)

    def forward(r, rows, begin, middle, last):
        tally[...] = jnp.zeros_like(tally)

        def parcels(i, carry):
            oy = far_first(i)
            for dx in (2, 1, 3, 0):
                s = slot_of(oy, dx)
                value = jnp.dot(
                    labels_t[pick_paper[s], :rows, :tile_rows], tiles[s], preferred_element_type=F32
                )
                if r == 0:
                    row = lax.broadcasted_iota(jnp.int32, value.shape, 0)
                    low = value - value.astype(BF16).astype(F32)
                    value = jnp.where(row == SEED_CLASSES + 1, low, value)
                parcel = value.astype(BF16)
                px[r, oy, dx, :rows] = parcel
                tally[:rows, :] += parcel.astype(F32) * jnp.where(s < count[0], 1.0, 0.0)
                if dx:
                    send(
                        px.at[r, oy, dx, pl.ds(0, rows)], xr.at[r, oy, dx - 1, pl.ds(0, rows)],
                        xs_send.at[r], xr_sem.at[r, oy], at(0, dx),
                    )
            return carry

        lax.fori_loop(0, NY, parcels, 0)
        begin()

        def row_sum(oy, t, span):
            s = slot_of(oy, 0)
            parts = [px[r, oy, 0, span]] + [xr[r, oy, dx - 1, span] for dx in range(1, NX)]
            return add(part.astype(F32) * weights[dx, t, s][:, :tile_cols] for dx, part in enumerate(parts))

        size = 64 if rows % 64 == 0 else 32
        parts = rows // size

        def hop(step):
            for part in range(parts):
                span = pl.ds(part * size, size)
                for way in range(2):
                    away = NY // 2 - step
                    oy = away if way == 0 else NY - away
                    if step == 0:
                        chosen = [way]
                    else:
                        chosen = [0, 1]
                        before = [way] if step == 1 else [0, 1]
                        drain(yin.at[r, way, step - 1, pl.ds(before[0], len(before)), span], yin_sem.at[r, way, step - 1, part])
                    if part == 0 and (step > 0 or way == 0):
                        drain(xr.at[r, oy, :, pl.ds(0, rows)], xr_sem.at[r, oy])
                    for t in chosen:
                        total = row_sum(oy, t, span)
                        if step > 0 and t in before:
                            total = total + yin[r, way, step - 1, t, span]
                        yout[r, way, step, t, span] = total
                    tiles_sent = pl.ds(chosen[0], len(chosen))
                    send(
                        yout.at[r, way, step, tiles_sent, span], yin.at[r, way, step, tiles_sent, span],
                        yout_send.at[r, way, step], yin_sem.at[r, way, step, part], at(1 if way == 0 else NY - 1, 0),
                    )

        hop(0)
        hop(1)
        middle()
        hop(2)
        hop(3)
        drain(xr.at[r, 0, :, pl.ds(0, rows)], xr_sem.at[r, 0])
        totals = [row_sum(0, t, pl.ds(0, rows)) for t in range(2)]
        first = last()
        for way in range(2):
            for part in range(parts):
                drain(yin.at[r, way, NY // 2 - 1, :, pl.ds(part * size, size)], yin_sem.at[r, way, NY // 2 - 1, part])
        for t, total in enumerate(totals):
            for way in range(2):
                total = total + yin[r, way, NY // 2 - 1, t, :rows]
            if r == 0:
                total = jnp.concatenate([total, jnp.zeros((classes - rows, tile_cols), F32)], axis=0)
            mass = total.T
            if r == 0:
                column = lax.broadcasted_iota(jnp.int32, mass.shape, 1)
                degree[pl.ds(t * tile_cols, tile_cols), :] = jnp.sum(
                    jnp.where(column >= SEED_CLASSES, mass, 0.0), axis=1, keepdims=True
                )
                mass = jnp.where(column >= SEED_CLASSES, 0.0, mass)
            k = mass + prior_ref[...]
            author_k[pl.ds(t * tile_cols, tile_cols), :] = k
            own[r, t] = k.astype(BF16)
        return first

    def mask_tiles():
        def row(oy, carry):
            for dx in range(NX):
                s = slot_of(oy, (NX - dx) % NX)
                live = jnp.where(s < count[0], 1.0, 0.0)
                for q in range(2):
                    keep = jnp.where(pick_paper[s] == q, live, 0.0)
                    keep = jnp.full((1, tile_cols), keep, F32).astype(BF16)
                    masked[q, oy, :, dx * tile_cols:(dx + 1) * tile_cols] = tiles[s] * keep
            return carry

        lax.fori_loop(0, NY, row, 0)

    def keep_seeds():
        for q in range(2):
            seeds[q] = one_hot(q).T[:tile_rows]

    def first_author_sum(r):
        mass = jnp.sum(tally[...].T, axis=0, keepdims=True)
        if r == 0:
            mass = jnp.where(lax.broadcasted_iota(jnp.int32, mass.shape, 1) >= SEED_CLASSES, 0.0, mass)
        return mass + 2.0 * tile_cols * prior_ref[...]

    def first_paper_sum(columns):
        k = author_k[...]
        share = rows_of(k, columns) * k * columns
        if final:
            author_out[...] = share
        return jnp.sum(degree[...] * share, axis=0, keepdims=True) + 2.0 * tile_rows * prior_ref[...]

    def pass_on(r, away):
        for way in range(2):
            here = own.at[r] if away == 1 else yb.at[r, (NY - away if way == 0 else away - 2)]
            there = yb.at[r, (NY - away - 1 if way == 0 else away - 1)]
            if away == NY // 2:
                here, there = here.at[pl.ds(way, 1)], there.at[pl.ds(way, 1)]
            oy = NY - away if way == 0 else away
            send(here, there, yb_send.at[r, way, away - 1], yb_sem.at[r, oy - 1], at(1 if way == 0 else NY - 1, 0))

    def spread(r, oy, both):
        s = slot_of(oy, 0)
        for dx in (2, 1, 3, 0):
            second = weights[(NX - dx) % NX, 2, s] > 0.5
            chosen = jnp.where(second, both[1].astype(F32), both[0].astype(F32))
            if dx:
                xs[r, oy, dx - 1] = chosen.astype(BF16)
                send(xs.at[r, oy, dx - 1], xa.at[r, oy, dx], xa_send.at[r], xa_sem.at[r, oy], at(0, dx))
            else:
                xa[r, oy, 0] = chosen.astype(BF16)

    def spread_from(r, away):
        for oy in (NY - away, away)[: 1 if away == NY // 2 else 2]:
            drain(yb.at[r, oy - 1], yb_sem.at[r, oy - 1])
        if away < NY // 2:
            pass_on(r, away + 1)
        for oy in (NY - away, away)[: 1 if away == NY // 2 else 2]:
            spread(r, oy, [yb[r, oy - 1, 0], yb[r, oy - 1, 1]])

    def paper_masses(r, columns, first, stop):
        def step(i, carry):
            oy = far_first(NY - 1 - i)
            drain(xa.at[r, oy, pl.ds(1, NX - 1)], xa_sem.at[r, oy])
            scaled = xa[r, oy].astype(F32).reshape(NX * tile_cols, classes) * columns
            share = (scaled * (1.0 / jnp.sum(scaled, axis=1, keepdims=True))).astype(BF16)
            for q in range(2):
                paper_k[q] += jnp.dot(masked[q, oy], share, preferred_element_type=F32)
            return carry

        lax.fori_loop(first, stop, step, 0)

    def sum_all(k, row):
        sum_start(k, row)
        sum_middle(k)
        return sum_end(k)

    def rows_of(k, columns):
        return 1.0 / jnp.sum(k * columns, axis=1, keepdims=True)

    def weighted_sum(blocks, columns):
        total = jnp.zeros((8, classes), F32)
        for block in blocks:
            k = block[...]
            total = total + jnp.sum((k * rows_of(k, columns)).reshape(-1, 8, classes), axis=0)
        return jnp.sum(total, axis=0, keepdims=True)

    author_blocks = [author_k.at[pl.ds(i, 64)] for i in range(0, 2 * tile_cols, 64)]
    paper_blocks = [paper_k.at[q, pl.ds(i, 64)] for q in range(2) for i in range(0, tile_rows, 64)]

    for r in range(ROUNDS):
        base = r * 2 * ITERS
        final = r == ROUNDS - 1

        def begin():
            sum_start(base, first_author_sum(r))
            if r == 0:
                drain(weights.at[pl.ds(1, NX - 1)], w_recv)

        columns = forward(
            r, SEED_ROWS if r == 0 else classes, begin, lambda: sum_middle(base), lambda: sum_end(base)
        )
        pass_on(r, 1)
        for i in range(1, ITERS):
            sum_start(base + i, weighted_sum(author_blocks, columns))
            if i == 1:
                spread(r, 0, [own[r, 0], own[r, 1]])
                if r == 0:
                    mask_tiles()
            else:
                spread_from(r, 2 * i - 2)
            sum_middle(base + i)
            if i < ITERS - 1:
                spread_from(r, 2 * i - 1)
            elif r == 0:
                keep_seeds()
            columns = sum_end(base + i)
        sum_start(base + ITERS, first_paper_sum(columns))
        for q in range(2):
            paper_k[q] = jnp.broadcast_to(prior_ref[...], (tile_rows, classes))
        paper_masses(r, columns, 0, NY // 2)
        sum_middle(base + ITERS)
        paper_masses(r, columns, NY // 2, NY)
        columns = sum_end(base + ITERS)

        def iterate(i, columns):
            return sum_all(base + ITERS + i, weighted_sum(paper_blocks, columns))

        columns = lax.fori_loop(1, ITERS, iterate, columns)
        for q in range(2):
            k = paper_k[q]
            updated = KEEP * (rows_of(k, columns) * k * columns) + (1.0 - KEEP) * seeds[q]
            if final:
                paper_out[pl.ds(q * tile_rows, tile_rows), :] = updated
            else:
                rounded = updated.astype(BF16).astype(F32)
                gap = jnp.zeros((code.shape[1] - tile_rows, classes), F32)
                labels_t[q] = jnp.concatenate([rounded, gap], axis=0).T.astype(BF16)

    drain(weights.at[pl.ds(1, NX - 1)], w_send)
    for r in range(ROUNDS):
        rows = SEED_ROWS if r == 0 else classes
        drain(xr.at[r, :, :, pl.ds(0, rows)], xs_send.at[r])
        for way in range(2):
            for step in range(NY // 2):
                sent_tiles = pl.ds(way, 1) if step == 0 else pl.ds(0, 2)
                drain(yout.at[r, way, step, sent_tiles, pl.ds(0, rows)], yout_send.at[r, way, step])
                last_hop = step == NY // 2 - 1
                drain(yb.at[r, 0, pl.ds(0, 1 if last_hop else 2)], yb_send.at[r, way, step])
        drain(xa.at[r, :, pl.ds(1, NX - 1)], xa_send.at[r])

    def sent(k, carry):
        drain(got1.at[k], ss1.at[k])
        drain(got2.at[k], ss2.at[k])
        return carry

    lax.fori_loop(0, ROUNDS * 2 * ITERS, sent, 0)


def scores(updated, share, paper_scores, author_scores):
    paper_scores[...] = updated.shape[1] * updated[...]
    author_scores[...] = share.shape[1] * share[...]


def on_device(
    tile_values, tile_paper, tile_author, tile_count, seed_class, train_mask, class_prior, class_target
):
    slots, tile_rows, tile_cols = tile_values.shape
    classes = class_prior.shape[0]
    padded = -(-tile_rows // 128) * 128
    smem, vmem = pl.BlockSpec(memory_space=pltpu.SMEM), pl.BlockSpec(memory_space=pltpu.VMEM)
    dma = pltpu.SemaphoreType.DMA
    sums = ROUNDS * 2 * ITERS
    tall, wide = (classes, tile_cols), (tile_cols, classes)
    updated, share = pl.pallas_call(
        kernel,
        out_shape=(
            jax.ShapeDtypeStruct((2 * tile_rows, classes), F32),
            jax.ShapeDtypeStruct((2 * tile_cols, classes), F32),
        ),
        in_specs=[pl.BlockSpec(memory_space=pl.ANY), smem, smem, smem, vmem, vmem, vmem],
        out_specs=(vmem, vmem),
        scratch_shapes=[
            pltpu.VMEM((slots, tile_rows, tile_cols), BF16),
            pltpu.VMEM((2, NY, tile_rows, NX * tile_cols), BF16),
            pltpu.VMEM((2, padded), jnp.int32),
            pltpu.VMEM((2, classes, padded), BF16),
            pltpu.VMEM((2, tile_rows, classes), F32),
            pltpu.VMEM(tall, F32),
            pltpu.VMEM((NX, 3, slots, 1, classes), F32),
            pltpu.VMEM((2 * tile_cols, 1), F32),
            pltpu.VMEM((2 * tile_cols, classes), F32),
            pltpu.VMEM((2, tile_rows, classes), F32),
            pltpu.VMEM((ROUNDS, NY, NX, *tall), BF16),
            pltpu.VMEM((ROUNDS, NY, NX - 1, *tall), BF16),
            pltpu.VMEM((ROUNDS, 2, NY // 2, 2, *tall), F32),
            pltpu.VMEM((ROUNDS, 2, NY // 2, 2, *tall), F32),
            pltpu.VMEM((ROUNDS, 2, *wide), BF16),
            pltpu.VMEM((ROUNDS, NY - 1, 2, *wide), BF16),
            pltpu.VMEM((ROUNDS, NY, NX - 1, *wide), BF16),
            pltpu.VMEM((ROUNDS, NY, NX, *wide), BF16),
            pltpu.VMEM((sums, 1, classes), F32),
            pltpu.VMEM((sums, len(ZC), 1, classes), F32),
            pltpu.VMEM((sums, 1, classes), F32),
            pltpu.VMEM((sums, len(YX), 1, classes), F32),
            dma(()), dma(()), dma(()),
            dma((ROUNDS, NY)), dma((ROUNDS,)), dma((ROUNDS, 2, NY // 2, 8)), dma((ROUNDS, 2, NY // 2)),
            dma((ROUNDS, NY - 1)), dma((ROUNDS, 2, NY // 2)), dma((ROUNDS, NY)), dma((ROUNDS,)),
            dma((sums,)), dma((sums,)), dma((sums,)), dma((sums,)),
        ],
        compiler_params=pltpu.CompilerParams(
            collective_id=0, has_side_effects=True, vmem_limit_bytes=56 * 1024 * 1024
        ),
        name="propagate",
    )(
        tile_values, tile_paper, tile_author, tile_count,
        jnp.where(train_mask == 1, seed_class, -1).reshape(2, tile_rows),
        class_prior.reshape(1, classes), class_target.reshape(1, classes),
    )
    return pl.pallas_call(
        scores,
        out_shape=(
            jax.ShapeDtypeStruct(updated.shape, F32),
            jax.ShapeDtypeStruct(share.shape, F32),
        ),
        name="scores",
    )(updated, share)


def solution(mesh):
    placed = (
        P(("grp", "blk"), None, None),
        P(("grp", "blk")),
        P(("grp", "blk")),
        P(("grp", "blk")),
        P(("grp", "blk")),
        P(("grp", "blk")),
        P(),
        P(),
    )
    return jax.shard_map(
        on_device,
        mesh=mesh,
        in_specs=placed,
        out_specs=(P(("grp", "blk"), None), P(("grp", "blk"), None)),
        check_vma=False,
    )
```
